128 devices in a mesh: chan: 8 (over z, core), rad: 16 (over y, x).
Axes of the slice: x: 4, y: 4, z: 4, core: 2. Of those that a mesh axis runs over, the one named last changes fastest.
Arguments:
- vectors: float32 [1, 2, 104, 512, 512], P(None, None, 'chan', 'rad'), may hold values from -6 to 6
- eigenvectors: float32 [2, 512, 512], replicated, may hold values from -0.1875 to 0.1875
- energies: float32 [512], replicated, may hold values from 0 to 2
- widths: float32 [512], replicated, may hold values from 0 to 1
- shift_energy: float32 [1], replicated, may hold values from 0.5 to 2
- shift_width: float32 [1], replicated, may hold values from 0.5 to 1
- slot_channel: int32 [104], replicated, may hold values from 0 to 103, as said below
- partners: int32 [104, 12], replicated, may hold values from 0 to 103
- multipole: int32 [104, 12], replicated, may hold values from 0 to 3
- counts: int32 [104], replicated, may hold values from 1 to 12, as said below
- angular: float32 [104, 12], replicated, may hold values from -12 to 12
Outputs:
- update: float32 [1, 2, 104, 512, 512], P(None, None, 'chan', 'rad')
The draws below stay inside these ranges and needn't reach their ends.
Inputs may be any that keep to these rules, and one draw needn't show every extreme that they name: `slot_channel`: a permutation of the channel numbers; slot s belongs to group s // 13. Entries at positions counts[c] and beyond of a channel's lists are ignored.
All inputs are finite; a program needn't handle non-finite values.
Results may differ from the reference program's by a relative error of at most 0.0024.
Values may be sent and summed in bfloat16 or wider, within the bound.
A program may use at most 64 MiB of HBM per device.

```python
import jax
import jax.numpy as jnp
from jax import lax

POINTS = 512
CHANNELS = 104
ORDERS = 4
LINKS = 12
VECTORS = 1
GROUP = 13


def draw_slot_channel(key, part):
    base = jax.random.fold_in(key, 11)
    order_key, inner_key = jax.random.split(base)
    groups = CHANNELS // GROUP
    group_order = jax.random.permutation(order_key, groups).astype(jnp.int32)
    scores = jax.random.randint(inner_key, (groups, GROUP), 0, 1 << 20) * GROUP + jnp.arange(GROUP, dtype=jnp.int32)[None, :]
    within = jnp.argsort(scores, axis=1).astype(jnp.int32)
    return (group_order[:, None] * GROUP + within).reshape(CHANNELS).astype(jnp.int32)


def draw_counts(key, part):
    noise = jax.random.randint(jax.random.fold_in(key, 5), (CHANNELS,), 0, 3)
    ids = jnp.arange(CHANNELS, dtype=jnp.int32)
    values = LINKS - ids * (LINKS - 2) // CHANNELS - noise
    values = jnp.clip(values, 1, LINKS)
    return jnp.where(ids == 0, LINKS, values).astype(jnp.int32)


def with_ends(result, own_key, least, largest):
    spot = [jax.random.randint(jax.random.fold_in(own_key, axis), (), 0, length) for axis, length in enumerate(result.shape)]
    widest = result.shape.index(max(result.shape))
    beside = spot[:widest] + [(spot[widest] + 1) % result.shape[widest]] + spot[widest + 1:]
    return result.at[tuple(spot)].set(least).at[tuple(beside)].set(largest)


def block_scale(key, extent, pieces, low, top_value):
    gain = 1.0
    for axis_at, blocks in pieces:
        heights = jax.random.uniform(jax.random.fold_in(jax.random.fold_in(key, 6), axis_at), (blocks,), jnp.float32, low / len(pieces), top_value / len(pieces))
        gain = gain * jnp.repeat(jnp.exp(heights), extent[axis_at] // blocks).reshape((-1,) + (1,) * (len(extent) - 1 - axis_at))
    return gain


def bell_draw(rng, shape, scale, bound, shards=(), kind=jnp.bfloat16):
    values = jax.random.normal(rng, shape, jnp.float32) * scale
    if len(shards) > 0:
        values = block_scale(rng, shape, shards, -0.22, 0.18) * values
    return jnp.clip(values, min=-bound, max=bound).astype(kind)


def setup_inputs(seed: int = 0) -> dict:
    streams_of = jax.random.split(jax.random.key(seed), 12)
    vectors = bell_draw(streams_of[0], (VECTORS, 2, CHANNELS, POINTS, POINTS), 1.0, 6.0, ((2, 8), (3, 16)), jnp.float32)
    eigenvectors = bell_draw(streams_of[1], (2, POINTS, POINTS), (2 * POINTS) ** -0.5, 0.1875, (), jnp.float32)
    energies = jnp.clip(jax.random.uniform(streams_of[2], (POINTS,), jnp.float32, 0.0, 2.0), 0.0, 2.0)
    widths = jnp.clip(jax.random.uniform(streams_of[3], (POINTS,), jnp.float32, 0.0, 1.0), 0.0, 1.0)
    shift_energy = jnp.clip(jax.random.uniform(streams_of[4], (1,), jnp.float32, 0.5, 2.0), 0.5, 2.0)
    shift_width = jnp.clip(jax.random.uniform(streams_of[5], (1,), jnp.float32, 0.5, 1.0), 0.5, 1.0)
    slot_channel = draw_slot_channel(jax.random.fold_in(streams_of[11], 71), 0)
    partners = with_ends(jax.random.randint(streams_of[7], (CHANNELS, LINKS), 0, CHANNELS), jax.random.fold_in(streams_of[7], 1), 0, CHANNELS - 1).astype(jnp.int32)
    multipole = with_ends(jax.random.randint(streams_of[8], (CHANNELS, LINKS), 0, ORDERS), jax.random.fold_in(streams_of[8], 1), 0, ORDERS - 1).astype(jnp.int32)
    counts = draw_counts(jax.random.fold_in(streams_of[11], 71), 0)
    angular = bell_draw(streams_of[10], (CHANNELS, LINKS), 2.0, 12.0, (), jnp.float32)
    return dict(vectors=vectors, eigenvectors=eigenvectors, energies=energies, widths=widths, shift_energy=shift_energy, shift_width=shift_width, slot_channel=slot_channel, partners=partners, multipole=multipole, counts=counts, angular=angular)


spacing = 0.01
first_point = 8.0
angle_ecs = 0.3
highest = lax.Precision.HIGHEST


def contour(index, points):
    start = (3 * points) // 4
    position = spacing * (index.astype(jnp.float32) + first_point)
    edge = spacing * (start + first_point)
    beyond = jnp.maximum(position - edge, 0.0)
    return (jnp.minimum(position, edge) + beyond * jnp.cos(angle_ecs), beyond * jnp.sin(angle_ecs))


def complex_product(first, second):
    return (first[0] * second[0] - first[1] * second[1], first[0] * second[1] + first[1] * second[0])


def kernels(row_index, col_index, points, orders):
    upper = contour(jnp.maximum(row_index[:, None], col_index[None, :]), points)
    lower = contour(jnp.minimum(row_index[:, None], col_index[None, :]), points)
    modulus = upper[0] * upper[0] + upper[1] * upper[1]
    inverse = (upper[0] / modulus, -upper[1] / modulus)
    ratio = complex_product(lower, inverse)
    real_list = [inverse[0]]
    imag_list = [inverse[1]]
    for order in range(1, orders):
        nextone = complex_product((real_list[-1], imag_list[-1]), ratio)
        real_list.append(nextone[0])
        imag_list.append(nextone[1])
    return (jnp.stack(real_list), jnp.stack(imag_list))


def transform(field, matrix, form):
    real_in = field[:, 0]
    imag_in = field[:, 1]
    out_real = jnp.einsum(form, real_in, matrix[0], precision=highest) - jnp.einsum(form, imag_in, matrix[1], precision=highest)
    out_imag = jnp.einsum(form, real_in, matrix[1], precision=highest) + jnp.einsum(form, imag_in, matrix[0], precision=highest)
    return jnp.stack([out_real, out_imag], axis=1)


def precondition(field, eigenvectors, factor):
    spectral = transform(field, eigenvectors, "nsra,ab->nsrb")
    spectral = transform(spectral, eigenvectors, "nsab,ai->nsib")
    scaled = jnp.stack(complex_product((spectral[:, 0], spectral[:, 1]), factor), axis=1)
    back = transform(scaled, eigenvectors, "nsib,ai->nsab")
    return transform(back, eigenvectors, "nsrb,ab->nsra")


def reference(vectors, eigenvectors, energies, widths, shift_energy, shift_width, slot_channel, partners, multipole, counts, angular):
    points = eigenvectors.shape[1]
    channels = slot_channel.shape[0]
    links = partners.shape[1]
    den_real = energies[:, None] + energies[None, :] - shift_energy[0]
    den_imag = -(widths[:, None] + widths[None, :]) - shift_width[0]
    modulus = den_real * den_real + den_imag * den_imag
    factor = (den_real / modulus, -den_imag / modulus)
    first = precondition(vectors, eigenvectors, factor)
    ids = jnp.arange(channels, dtype=jnp.int32)
    slot_of = jnp.zeros((channels,), jnp.int32).at[slot_channel].set(ids)
    live = jnp.arange(links, dtype=jnp.int32)[None, :] < counts[:, None]
    weight = jnp.where(live, angular, 0.0).astype(jnp.float32)
    target = jnp.broadcast_to(slot_of[:, None], (channels, links))
    source = slot_of[partners]
    coupling = jnp.zeros((ORDERS, channels, channels), jnp.float32).at[multipole, target, source].add(weight)
    coupled_in = lax.optimization_barrier(first.astype(jnp.bfloat16))
    widened = coupled_in.astype(jnp.float32)
    grid = jnp.arange(points, dtype=jnp.int32)
    table = kernels(grid, grid, points, ORDERS)
    total_real = jnp.zeros(first[:, 0].shape, jnp.float32)
    total_imag = jnp.zeros(first[:, 0].shape, jnp.float32)
    for order in range(ORDERS):
        mixed = jnp.einsum("st,nqtab->nqsab", coupling[order], widened, precision=highest)
        added = complex_product((table[0][order], table[1][order]), (mixed[:, 0], mixed[:, 1]))
        total_real = total_real + added[0]
        total_imag = total_imag + added[1]
    coupled = jnp.stack([total_real, total_imag], axis=1)
    return first - precondition(coupled, eigenvectors, factor)
```

```python
import math

import jax
import jax.numpy as jnp
from jax import lax
from jax.experimental import pallas as pl
from jax.experimental.pallas import tpu as pltpu
from jax.sharding import PartitionSpec as P

F32 = jnp.float32
BF16 = jnp.bfloat16
MESH = pl.DeviceIdType.MESH
POINTS = 512
CHANNELS = 104
GROUP = 13
ORDERS = 4
LINKS = 12
NCHAN = 8
NRAD = 16
DEVICES = NCHAN * NRAD
ROWS = POINTS // NRAD
HALF = POINTS
FULL = 2 * POINTS

spacing = 0.01
first_point = 8.0
angle_ecs = 0.3


def dot(a, b):
    return jnp.dot(a, b, preferred_element_type=F32)


def split(x):
    hi = x.astype(BF16)
    return hi, (x - hi.astype(F32)).astype(BF16)


def complex_product(a, b):
    return (a[0] * b[0] - a[1] * b[1], a[0] * b[1] + a[1] * b[0])


def kernel(
    vec,
    eig,
    energies,
    widths,
    shift_energy,
    shift_width,
    slot_channel,
    slot_of,
    partners,
    multipole,
    counts,
    angular,
    out,
    xin,
    wr,
    wrt,
    wl,
    wlt,
    fac,
    yh,
    yl,
    zh,
    zl,
    a1,
    fb,
    got,
    csend,
    crecv,
    dsend,
    drecv,
    table,
    t1s,
    t1r,
    t2s,
    t2r,
    t3s,
    t3r,
    t4s,
    t4r,
):
    chan = lax.axis_index("chan")
    rad = lax.axis_index("rad")
    has_slot = rad < GROUP
    my_slot = chan * GROUP + rad
    my_block = rad * NCHAN + chan
    plane = rad // 4

    barrier = pltpu.get_barrier_semaphore()

    @pl.loop(0, DEVICES)
    def _(d):
        to_rad = d // NCHAN
        to_chan = d % NCHAN

        @pl.when(d != my_block)
        def _():
            pl.semaphore_signal(barrier, inc=1, device_id=(to_chan, to_rad), device_id_type=MESH)

    pl.semaphore_wait(barrier, DEVICES - 1)

    my_rows = pl.ds(pl.multiple_of(rad * ROWS, ROWS), ROWS)

    @pl.loop(0, NRAD)
    def _(k):
        s = (rad + 1 + k) % NRAD

        @pl.when(jnp.logical_and(s < GROUP, s != rad))
        def _():
            pltpu.make_async_remote_copy(
                src_ref=vec.at[0, :, s],
                dst_ref=xin.at[:, my_rows],
                send_sem=t1s,
                recv_sem=t1r.at[rad],
                device_id=(chan, s),
                device_id_type=MESH,
            ).start()

    @pl.when(has_slot)
    def _():
        pltpu.make_async_copy(vec.at[0, :, rad], xin.at[:, my_rows], t1r.at[rad]).start()

    @pl.loop(0, 4)
    def _(g):
        rows = pl.ds(pl.multiple_of(g * 128, 128), 128)
        low = pl.ds(pl.multiple_of(HALF + g * 128, 128), 128)
        ur = eig[0, rows, :]
        ui = eig[1, rows, :]
        for part, (r, i) in enumerate(zip(split(ur), split(ui))):
            wr[part, rows, 0:HALF] = r
            wr[part, rows, HALF:FULL] = i
            wr[part, low, 0:HALF] = -i
            wr[part, low, HALF:FULL] = r
            wl[part, rows, 0:HALF] = r
            wl[part, rows, HALF:FULL] = -i
            wl[part, low, 0:HALF] = i
            wl[part, low, HALF:FULL] = r
        tr = eig[0, :, rows].T
        ti = eig[1, :, rows].T
        for part, (r, i) in enumerate(zip(split(tr), split(ti))):
            wrt[part, rows, 0:HALF] = r
            wrt[part, rows, HALF:FULL] = i
            wrt[part, low, 0:HALF] = -i
            wrt[part, low, HALF:FULL] = r
            wlt[part, rows, 0:HALF] = r
            wlt[part, rows, HALF:FULL] = -i
            wlt[part, low, 0:HALF] = i
            wlt[part, low, HALF:FULL] = r
        e_row = jnp.broadcast_to(energies[0:1, :], (128, POINTS))
        w_row = jnp.broadcast_to(widths[0:1, :], (128, POINTS))
        e_col = jnp.broadcast_to(energies[0:1, rows], (POINTS, 128)).T
        w_col = jnp.broadcast_to(widths[0:1, rows], (POINTS, 128)).T
        den_real = e_col + e_row - shift_energy[0]
        den_imag = -(w_col + w_row) - shift_width[0]
        modulus = den_real * den_real + den_imag * den_imag
        fac[0, rows, :] = den_real / modulus
        fac[1, rows, :] = -den_imag / modulus

    row = my_block // 4 * 16 + lax.broadcasted_iota(jnp.int32, (16, 128), 0)
    col = my_block % 4 * 128 + lax.broadcasted_iota(jnp.int32, (16, 128), 1)

    def bent(index):
        start = 3 * POINTS // 4
        position = spacing * (index.astype(F32) + first_point)
        edge = spacing * (start + first_point)
        beyond = jnp.maximum(position - edge, 0.0)
        return (jnp.minimum(position, edge) + beyond * math.cos(angle_ecs), beyond * math.sin(angle_ecs))

    upper = bent(jnp.maximum(row, col))
    lower = bent(jnp.minimum(row, col))
    modulus = upper[0] * upper[0] + upper[1] * upper[1]
    inverse = (upper[0] / modulus, -upper[1] / modulus)
    ratio = complex_product(lower, inverse)
    now = inverse
    for order in range(ORDERS):
        table[order, 0] = now[0]
        table[order, 1] = now[1]
        now = complex_product(now, ratio)

    def left_pair(weights, right_h, right_l, m, size):
        rows = pl.ds(pl.multiple_of(m * size, size), size)
        low = pl.ds(pl.multiple_of(HALF + m * size, size), size)
        result = []
        for r in (rows, low):
            h = weights[0, r, :]
            lo = weights[1, r, :]
            result.append(dot(h, right_h[...]) + dot(h, right_l[...]) + dot(lo, right_h[...]))
        return result

    def scaled_left(m):
        size = 256
        rows = pl.ds(pl.multiple_of(m * size, size), size)
        low = pl.ds(pl.multiple_of(HALF + m * size, size), size)
        re, im = left_pair(wlt, yh, yl, m, size)
        z = complex_product((re, im), (fac[0, rows, :], fac[1, rows, :]))
        for r, v in zip((rows, low), z):
            h, lo = split(v)
            zh[r, :] = h
            zl[r, :] = lo

    def store_y(g, y):
        rows = pl.ds(pl.multiple_of(g * 128, 128), 128)
        low = pl.ds(pl.multiple_of(HALF + g * 128, 128), 128)
        h, lo = split(y)
        yh[rows, :] = h[:, 0:HALF]
        yh[low, :] = h[:, HALF:FULL]
        yl[rows, :] = lo[:, 0:HALF]
        yl[low, :] = lo[:, HALF:FULL]

    @pl.when(has_slot)
    def _():
        @pl.loop(0, 4)
        def _(k):
            g = (plane + k) % 4

            @pl.loop(0, 4)
            def _(q):
                src = 4 * g + q
                part = xin.at[:, pl.ds(pl.multiple_of(src * ROWS, ROWS), ROWS)]
                pltpu.make_async_copy(part, part, t1r.at[src]).wait()

            rows = pl.ds(pl.multiple_of(g * 128, 128), 128)
            x = jnp.concatenate([xin[0, rows, :], xin[1, rows, :]], axis=1)
            h, lo = split(x)
            store_y(g, dot(h, wr[0]) + dot(h, wr[1]) + dot(lo, wr[0]))

        @pl.loop(0, 2)
        def _(m):
            scaled_left(m)

        @pl.loop(0, 4)
        def _(k):
            m = (plane + 1 + k) % 4
            rows = pl.ds(pl.multiple_of(m * 128, 128), 128)
            re, im = left_pair(wl, zh, zl, m, 128)
            a1[0, rows, :] = re
            a1[1, rows, :] = im
            h, lo = split(jnp.concatenate([re, im], axis=1))
            f = (dot(h, wrt[0]) + dot(h, wrt[1]) + dot(lo, wrt[0])).astype(BF16)
            for ii in range(8):
                for j in range(4):
                    for ri in range(2):
                        at = HALF * ri + 128 * j
                        fb[32 * m + 4 * ii + j, ri] = f[16 * ii : 16 * ii + 16, at : at + 128]

            @pl.loop(0, 32)
            def _(q):
                d = 32 * m + q

                @pl.when(d == my_block)
                def _():
                    pltpu.make_async_copy(fb.at[d], got.at[my_slot], t2r).start()

                @pl.when(d != my_block)
                def _():
                    pltpu.make_async_remote_copy(
                        src_ref=fb.at[d],
                        dst_ref=got.at[my_slot],
                        send_sem=t2s,
                        recv_sem=t2r,
                        device_id=(d % NCHAN, d // NCHAN),
                        device_id_type=MESH,
                    ).start()

    pltpu.make_async_copy(got, got, t2r).wait()

    @pl.loop(0, CHANNELS)
    def _(k):
        s = (my_slot + 1 + k) % CHANNELS
        c = slot_channel[s]
        live = counts[c]
        re = jnp.zeros((16, 128), F32)
        im = jnp.zeros((16, 128), F32)
        for p in range(LINKS):
            w = jnp.where(p < live, angular[c, p], 0.0)
            order = multipole[c, p]
            t = slot_of[0, partners[c, p]]
            gr = w * table[order, 0]
            gi = w * table[order, 1]
            vr = got[t, 0].astype(F32)
            vi = got[t, 1].astype(F32)
            re = re + (gr * vr - gi * vi)
            im = im + (gr * vi + gi * vr)
        csend[s, 0] = re.astype(BF16)
        csend[s, 1] = im.astype(BF16)

        to_chan = s // GROUP
        to_rad = s % GROUP
        same = to_rad * NCHAN + to_chan == my_block

        @pl.when(same)
        def _():
            pltpu.make_async_copy(csend.at[s], crecv.at[my_block], t3r.at[my_block // 32]).start()

        @pl.when(jnp.logical_not(same))
        def _():
            pltpu.make_async_remote_copy(
                src_ref=csend.at[s],
                dst_ref=crecv.at[my_block],
                send_sem=t3s,
                recv_sem=t3r.at[my_block // 32],
                device_id=(to_chan, to_rad),
                device_id_type=MESH,
            ).start()

    @pl.when(has_slot)
    def _():
        @pl.loop(0, 4)
        def _(k):
            m = (plane + k) % 4
            part = crecv.at[pl.ds(pl.multiple_of(32 * m, 32), 32)]
            pltpu.make_async_copy(part, part, t3r.at[m]).wait()
            cols = []
            for ri in range(2):
                for j in range(4):
                    cols.append(jnp.concatenate([crecv[32 * m + 4 * ii + j, ri] for ii in range(8)], axis=0))
            x = jnp.concatenate(cols, axis=1)
            store_y(m, dot(x, wr[0]) + dot(x, wr[1]))

        @pl.loop(0, 2)
        def _(m):
            scaled_left(m)

        @pl.loop(0, 4)
        def _(k):
            m = (plane + 1 + k) % 4
            rows = pl.ds(pl.multiple_of(m * 128, 128), 128)
            re, im = left_pair(wl, zh, zl, m, 128)
            for ri, v in enumerate((re, im)):
                diff = (a1[ri, rows, :] - v).astype(BF16)
                for q in range(4):
                    dsend[4 * m + q, ri] = diff[ROWS * q : ROWS * q + ROWS, :]

            @pl.loop(0, 4)
            def _(q):
                r = 4 * m + q

                @pl.when(r == rad)
                def _():
                    pltpu.make_async_copy(dsend.at[r], drecv.at[rad], t4r).start()

                @pl.when(r != rad)
                def _():
                    pltpu.make_async_remote_copy(
                        src_ref=dsend.at[r],
                        dst_ref=drecv.at[rad],
                        send_sem=t4s,
                        recv_sem=t4r,
                        device_id=(chan, r),
                        device_id_type=MESH,
                    ).start()

    pltpu.make_async_copy(drecv, drecv, t4r).wait()

    x = jnp.concatenate(
        [drecv[:, 0].reshape(GROUP * ROWS, POINTS), drecv[:, 1].reshape(GROUP * ROWS, POINTS)], axis=1
    )

    @pl.loop(0, 2)
    def _(ri):
        cols = pl.ds(pl.multiple_of(HALF * ri, HALF), HALF)
        u = dot(x, wrt[0, :, cols]) + dot(x, wrt[1, :, cols])
        out[0, ri] = u.reshape(GROUP, ROWS, POINTS)

    @pl.when(has_slot)
    def _():
        a = xin.at[:, pl.ds(0, (GROUP - 1) * ROWS)]
        pltpu.make_async_copy(a, a, t1s).wait()
        b = fb.at[pl.ds(0, DEVICES - 1)]
        pltpu.make_async_copy(b, b, t2s).wait()
        c = csend.at[pl.ds(0, CHANNELS - 1)]
        pltpu.make_async_copy(c, c, t3s).wait()
        d = dsend.at[pl.ds(0, NRAD - 1)]
        pltpu.make_async_copy(d, d, t4s).wait()

    @pl.when(jnp.logical_not(has_slot))
    def _():
        a = xin.at[:, pl.ds(0, GROUP * ROWS)]
        pltpu.make_async_copy(a, a, t1s).wait()
        pltpu.make_async_copy(csend, csend, t3s).wait()


def local(
    vectors,
    eigenvectors,
    energies,
    widths,
    shift_energy,
    shift_width,
    slot_channel,
    partners,
    multipole,
    counts,
    angular,
):
    slot_ids = jnp.arange(CHANNELS, dtype=jnp.int32)
    slot_of = jnp.sum(jnp.where(slot_channel[:, None] == slot_ids[None, :], slot_ids[:, None], 0), axis=0)
    vmem = pl.BlockSpec(memory_space=pltpu.VMEM)
    smem = pl.BlockSpec(memory_space=pltpu.SMEM)
    dma = pltpu.SemaphoreType.DMA
    return pl.pallas_call(
        kernel,
        name="step",
        out_shape=jax.ShapeDtypeStruct(vectors.shape, F32),
        in_specs=[pl.BlockSpec(memory_space=pl.ANY), vmem, vmem, vmem] + [smem] * 8,
        out_specs=vmem,
        scratch_shapes=[
            pltpu.VMEM((2, POINTS, POINTS), F32),
            pltpu.VMEM((2, FULL, FULL), BF16),
            pltpu.VMEM((2, FULL, FULL), BF16),
            pltpu.VMEM((2, FULL, FULL), BF16),
            pltpu.VMEM((2, FULL, FULL), BF16),
            pltpu.VMEM((2, POINTS, POINTS), F32),
            pltpu.VMEM((FULL, POINTS), BF16),
            pltpu.VMEM((FULL, POINTS), BF16),
            pltpu.VMEM((FULL, POINTS), BF16),
            pltpu.VMEM((FULL, POINTS), BF16),
            pltpu.VMEM((2, POINTS, POINTS), F32),
            pltpu.VMEM((DEVICES, 2, 16, 128), BF16),
            pltpu.VMEM((CHANNELS, 2, 16, 128), BF16),
            pltpu.VMEM((CHANNELS, 2, 16, 128), BF16),
            pltpu.VMEM((DEVICES, 2, 16, 128), BF16),
            pltpu.VMEM((NRAD, 2, ROWS, POINTS), BF16),
            pltpu.VMEM((GROUP, 2, ROWS, POINTS), BF16),
            pltpu.VMEM((ORDERS, 2, 16, 128), F32),
            dma,
            dma((NRAD,)),
            dma,
            dma,
            dma,
            dma((4,)),
            dma,
            dma,
        ],
        compiler_params=pltpu.CompilerParams(
            collective_id=0, has_side_effects=True, vmem_limit_bytes=62 * 1024 * 1024
        ),
    )(
        vectors,
        eigenvectors,
        energies.reshape(1, POINTS),
        widths.reshape(1, POINTS),
        shift_energy,
        shift_width,
        slot_channel,
        slot_of.reshape(1, CHANNELS),
        partners,
        multipole,
        counts,
        angular,
    )


def solution(mesh):
    spread = P(None, None, "chan", "rad", None)
    return jax.shard_map(
        local,
        mesh=mesh,
        in_specs=(spread,) + (P(),) * 10,
        out_specs=spread,
        check_vma=False,
    )
```

```python
import math

import jax
import jax.numpy as jnp
from jax import lax
from jax.experimental import pallas as pl
from jax.experimental.pallas import tpu as pltpu
from jax.sharding import PartitionSpec as P

F32 = jnp.float32
BF16 = jnp.bfloat16
MESH = pl.DeviceIdType.MESH
POINTS = 512
CHANNELS = 104
GROUP = 13
ORDERS = 4
LINKS = 12
NCHAN = 8
NRAD = 16
DEVICES = NCHAN * NRAD
ROWS = POINTS // NRAD
HALF = POINTS
FULL = 2 * POINTS

spacing = 0.01
first_point = 8.0
angle_ecs = 0.3


def dot(a, b):
    return jnp.dot(a, b, preferred_element_type=F32)


def split(x):
    hi = x.astype(BF16)
    return hi, (x - hi.astype(F32)).astype(BF16)


def complex_product(a, b):
    return (a[0] * b[0] - a[1] * b[1], a[0] * b[1] + a[1] * b[0])


def kernel(
    vec,
    eig,
    energies,
    widths,
    shift_energy,
    shift_width,
    slot_channel,
    slot_of,
    partners_in,
    multipole_in,
    counts,
    angular_in,
    out,
    xin,
    wr,
    wrt,
    wl,
    wlt,
    fac,
    yh,
    yl,
    zh,
    zl,
    a1,
    fb,
    got,
    csend,
    crecv,
    dsend,
    drecv,
    table,
    t1s,
    t1r,
    t2s,
    t2r,
    t3s,
    t3r,
    t4s,
    t4r,
    ready,
    partners,
    multipole,
    angular,
    tab,
):
    chan = lax.axis_index("chan")
    rad = lax.axis_index("rad")
    seat = (rad + 5 * (chan % 2)) % NRAD
    has_slot = jnp.logical_or(seat % 5 != 0, seat == 0)
    my_place = seat - seat // 5
    my_slot = chan * GROUP + my_place

    def place_of(to_chan, to_rad):
        to_seat = (to_rad + 5 * (to_chan % 2)) % NRAD
        return jnp.logical_or(to_seat % 5 != 0, to_seat == 0), to_seat - to_seat // 5

    def rad_of(to_chan, place):
        to_seat = place + jnp.where(place >= 5, 1, 0) + jnp.where(place >= 9, 1, 0)
        return (to_seat + 11 * (to_chan % 2)) % NRAD

    my_block = 32 * ((rad // 4 + rad % 4) % 4) + NCHAN * (rad % 4) + chan
    plane = rad // 4

    my_rows = pl.ds(pl.multiple_of(rad * ROWS, ROWS), ROWS)

    def left_pair(weights, right_h, right_l, m, size):
        rows = pl.ds(pl.multiple_of(m * size, size), size)
        low = pl.ds(pl.multiple_of(HALF + m * size, size), size)
        result = []
        for r in (rows, low):
            h = weights[0, r, :]
            lo = weights[1, r, :]
            result.append(dot(h, right_h[...]) + dot(h, right_l[...]) + dot(lo, right_h[...]))
        return result

    def scaled_left(m):
        size = 256
        rows = pl.ds(pl.multiple_of(m * size, size), size)
        low = pl.ds(pl.multiple_of(HALF + m * size, size), size)
        re, im = left_pair(wlt, yh, yl, m, size)
        z = complex_product((re, im), (fac[0, rows, :], fac[1, rows, :]))
        for r, v in zip((rows, low), z):
            h, lo = split(v)
            zh[r, :] = h
            zl[r, :] = lo

    def store_y(g, y):
        rows = pl.ds(pl.multiple_of(g * 128, 128), 128)
        low = pl.ds(pl.multiple_of(HALF + g * 128, 128), 128)
        h, lo = split(y)
        yh[rows, :] = h[:, 0:HALF]
        yh[low, :] = h[:, HALF:FULL]
        yl[rows, :] = lo[:, 0:HALF]
        yl[low, :] = lo[:, HALF:FULL]

    barrier = pltpu.get_barrier_semaphore()

    def greet():
        @pl.loop(1, NRAD)
        def _(k):
            to_rad = (rad + k) % NRAD
            pl.semaphore_signal(barrier, inc=1, device_id=(chan, to_rad), device_id_type=MESH)

        @pl.loop(1, NCHAN)
        def _(k):
            to_chan = (chan + k) % NCHAN
            pl.semaphore_signal(barrier, inc=1, device_id=(to_chan, rad), device_id_type=MESH)

        pl.semaphore_wait(barrier, NRAD + NCHAN - 2)

        @pl.loop(1, NCHAN)
        def _(k):
            to_chan = (chan + k) % NCHAN
            pl.semaphore_signal(ready, inc=1, device_id=(to_chan, rad), device_id_type=MESH)

    def send_rows():
        @pl.loop(0, NRAD)
        def _(k):
            s = (rad + 1 + k) % NRAD
            taken, place = place_of(chan, s)

            @pl.when(jnp.logical_and(taken, s != rad))
            def _():
                pltpu.make_async_remote_copy(
                    src_ref=vec.at[0, :, place],
                    dst_ref=xin.at[:, my_rows],
                    send_sem=t1s,
                    recv_sem=t1r.at[rad],
                    device_id=(chan, s),
                    device_id_type=MESH,
                ).start()

        @pl.when(has_slot)
        def _():
            pltpu.make_async_copy(vec.at[0, :, my_place], xin.at[:, my_rows], t1r.at[rad]).start()

    def all_ready():
        pl.semaphore_wait(ready, NCHAN - 1)

    def tables():
        return [
            pltpu.make_async_copy(partners_in, partners, tab.at[0]),
            pltpu.make_async_copy(multipole_in, multipole, tab.at[1]),
            pltpu.make_async_copy(angular_in, angular, tab.at[2]),
        ]

    def prepare():
        for copy in tables():
            copy.start()

        @pl.loop(0, 4)
        def _(g):
            rows = pl.ds(pl.multiple_of(g * 128, 128), 128)
            low = pl.ds(pl.multiple_of(HALF + g * 128, 128), 128)
            ur = eig[0, rows, :]
            ui = eig[1, rows, :]
            for part, (r, i) in enumerate(zip(split(ur), split(ui))):
                wr[part, rows, 0:HALF] = r
                wr[part, rows, HALF:FULL] = i
                wr[part, low, 0:HALF] = -i
                wr[part, low, HALF:FULL] = r
                wl[part, rows, 0:HALF] = r
                wl[part, rows, HALF:FULL] = -i
                wl[part, low, 0:HALF] = i
                wl[part, low, HALF:FULL] = r
            tr = eig[0, :, rows].T
            ti = eig[1, :, rows].T
            for part, (r, i) in enumerate(zip(split(tr), split(ti))):
                wrt[part, rows, 0:HALF] = r
                wrt[part, rows, HALF:FULL] = i
                wrt[part, low, 0:HALF] = -i
                wrt[part, low, HALF:FULL] = r
                wlt[part, rows, 0:HALF] = r
                wlt[part, rows, HALF:FULL] = -i
                wlt[part, low, 0:HALF] = i
                wlt[part, low, HALF:FULL] = r
            e_row = jnp.broadcast_to(energies[0:1, :], (128, POINTS))
            w_row = jnp.broadcast_to(widths[0:1, :], (128, POINTS))
            e_col = jnp.broadcast_to(energies[0:1, rows], (POINTS, 128)).T
            w_col = jnp.broadcast_to(widths[0:1, rows], (POINTS, 128)).T
            den_real = e_col + e_row - shift_energy[0]
            den_imag = -(w_col + w_row) - shift_width[0]
            modulus = den_real * den_real + den_imag * den_imag
            fac[0, rows, :] = den_real / modulus
            fac[1, rows, :] = -den_imag / modulus

        row = my_block // 4 * 16 + lax.broadcasted_iota(jnp.int32, (16, 128), 0)
        col = my_block % 4 * 128 + lax.broadcasted_iota(jnp.int32, (16, 128), 1)

        def bent(index):
            start = 3 * POINTS // 4
            position = spacing * (index.astype(F32) + first_point)
            edge = spacing * (start + first_point)
            beyond = jnp.maximum(position - edge, 0.0)
            return (jnp.minimum(position, edge) + beyond * math.cos(angle_ecs), beyond * math.sin(angle_ecs))

        upper = bent(jnp.maximum(row, col))
        lower = bent(jnp.minimum(row, col))
        modulus = upper[0] * upper[0] + upper[1] * upper[1]
        inverse = (upper[0] / modulus, -upper[1] / modulus)
        ratio = complex_product(lower, inverse)
        now = inverse
        for order in range(ORDERS):
            table[order, 0] = now[0]
            table[order, 1] = now[1]
            now = complex_product(now, ratio)

    def first_pass():
        @pl.when(has_slot)
        def _():
            @pl.loop(0, 4)
            def _(k):
                g = (plane + k) % 4

                @pl.loop(0, 4)
                def _(q):
                    src = 4 * g + q
                    part = xin.at[:, pl.ds(pl.multiple_of(src * ROWS, ROWS), ROWS)]
                    pltpu.make_async_copy(part, part, t1r.at[src]).wait()

                rows = pl.ds(pl.multiple_of(g * 128, 128), 128)
                x = jnp.concatenate([xin[0, rows, :], xin[1, rows, :]], axis=1)
                h, lo = split(x)
                store_y(g, dot(h, wr[0]) + dot(h, wr[1]) + dot(lo, wr[0]))

            @pl.loop(0, 2)
            def _(m):
                scaled_left(m)

            @pl.loop(0, 4)
            def _(k):
                m = (plane + 1 + k) % 4
                rows = pl.ds(pl.multiple_of(m * 128, 128), 128)
                re, im = left_pair(wl, zh, zl, m, 128)
                a1[0, rows, :] = re
                a1[1, rows, :] = im
                h, lo = split(jnp.concatenate([re, im], axis=1))
                f = (dot(h, wrt[0]) + dot(h, wrt[1]) + dot(lo, wrt[0])).astype(BF16)
                for ii in range(8):
                    for j in range(4):
                        for ri in range(2):
                            at = HALF * ri + 128 * j
                            fb[32 * m + 4 * ii + j, ri] = f[16 * ii : 16 * ii + 16, at : at + 128]

                @pl.loop(0, 32)
                def _(q):
                    d = 32 * m + q

                    @pl.when(d == my_block)
                    def _():
                        pltpu.make_async_copy(fb.at[d], got.at[my_slot], t2r).start()

                    @pl.when(d != my_block)
                    def _():
                        pltpu.make_async_remote_copy(
                            src_ref=fb.at[d],
                            dst_ref=got.at[my_slot],
                            send_sem=t2s,
                            recv_sem=t2r,
                            device_id=(q % NCHAN, 4 * ((m + 4 - q // NCHAN) % 4) + q // NCHAN),
                            device_id_type=MESH,
                        ).start()

    def couple():
        pltpu.make_async_copy(got, got, t2r).wait()

        @pl.loop(0, CHANNELS)
        def _(k):
            s = (my_slot + 1 + k) % CHANNELS
            c = slot_channel[s]
            live = counts[c]
            re = jnp.zeros((16, 128), F32)
            im = jnp.zeros((16, 128), F32)
            for p in range(LINKS):
                w = jnp.where(p < live, angular[c, p], 0.0)
                order = multipole[c, p]
                t = slot_of[0, partners[c, p]]
                gr = w * table[order, 0]
                gi = w * table[order, 1]
                vr = got[t, 0].astype(F32)
                vi = got[t, 1].astype(F32)
                re = re + (gr * vr - gi * vi)
                im = im + (gr * vi + gi * vr)
            csend[s, 0] = re.astype(BF16)
            csend[s, 1] = im.astype(BF16)

            to_chan = s // GROUP
            to_rad = rad_of(to_chan, s % GROUP)
            same = jnp.logical_and(to_rad == rad, to_chan == chan)

            @pl.when(same)
            def _():
                pltpu.make_async_copy(csend.at[s], crecv.at[my_block], t3r.at[my_block // 32]).start()

            @pl.when(jnp.logical_not(same))
            def _():
                pltpu.make_async_remote_copy(
                    src_ref=csend.at[s],
                    dst_ref=crecv.at[my_block],
                    send_sem=t3s,
                    recv_sem=t3r.at[my_block // 32],
                    device_id=(to_chan, to_rad),
                    device_id_type=MESH,
                ).start()

    def second_pass():
        @pl.when(has_slot)
        def _():
            @pl.loop(0, 4)
            def _(k):
                m = (plane + k) % 4
                part = crecv.at[pl.ds(pl.multiple_of(32 * m, 32), 32)]
                pltpu.make_async_copy(part, part, t3r.at[m]).wait()
                cols = []
                for ri in range(2):
                    for j in range(4):
                        cols.append(jnp.concatenate([crecv[32 * m + 4 * ii + j, ri] for ii in range(8)], axis=0))
                x = jnp.concatenate(cols, axis=1)
                store_y(m, dot(x, wr[0]) + dot(x, wr[1]))

            @pl.loop(0, 2)
            def _(m):
                scaled_left(m)

            @pl.loop(0, 4)
            def _(k):
                m = (plane + 1 + k) % 4
                rows = pl.ds(pl.multiple_of(m * 128, 128), 128)
                re, im = left_pair(wl, zh, zl, m, 128)
                for ri, v in enumerate((re, im)):
                    diff = (a1[ri, rows, :] - v).astype(BF16)
                    for q in range(4):
                        dsend[4 * m + q, ri] = diff[ROWS * q : ROWS * q + ROWS, :]

                @pl.loop(0, 4)
                def _(q):
                    r = 4 * m + q

                    @pl.when(r == rad)
                    def _():
                        pltpu.make_async_copy(dsend.at[r], drecv.at[my_place], t4r).start()

                    @pl.when(r != rad)
                    def _():
                        pltpu.make_async_remote_copy(
                            src_ref=dsend.at[r],
                            dst_ref=drecv.at[my_place],
                            send_sem=t4s,
                            recv_sem=t4r,
                            device_id=(chan, r),
                            device_id_type=MESH,
                        ).start()

    def finish():
        pltpu.make_async_copy(drecv, drecv, t4r).wait()

        x = jnp.concatenate(
            [drecv[:, 0].reshape(GROUP * ROWS, POINTS), drecv[:, 1].reshape(GROUP * ROWS, POINTS)], axis=1
        )

        @pl.loop(0, 2)
        def _(ri):
            cols = pl.ds(pl.multiple_of(HALF * ri, HALF), HALF)
            u = dot(x, wrt[0, :, cols]) + dot(x, wrt[1, :, cols])
            out[0, ri] = u.reshape(GROUP, ROWS, POINTS)

    def drain():
        @pl.when(has_slot)
        def _():
            a = xin.at[:, pl.ds(0, (GROUP - 1) * ROWS)]
            pltpu.make_async_copy(a, a, t1s).wait()
            b = fb.at[pl.ds(0, DEVICES - 1)]
            pltpu.make_async_copy(b, b, t2s).wait()
            c = csend.at[pl.ds(0, CHANNELS - 1)]
            pltpu.make_async_copy(c, c, t3s).wait()
            d = dsend.at[pl.ds(0, NRAD - 1)]
            pltpu.make_async_copy(d, d, t4s).wait()

        @pl.when(jnp.logical_not(has_slot))
        def _():
            a = xin.at[:, pl.ds(0, GROUP * ROWS)]
            pltpu.make_async_copy(a, a, t1s).wait()
            pltpu.make_async_copy(csend, csend, t3s).wait()

    greet()
    send_rows()
    prepare()
    all_ready()
    for copy in tables():
        copy.wait()
    first_pass()
    couple()
    second_pass()
    finish()
    drain()


def local(
    vectors,
    eigenvectors,
    energies,
    widths,
    shift_energy,
    shift_width,
    slot_channel,
    partners,
    multipole,
    counts,
    angular,
):
    slot_ids = jnp.arange(CHANNELS, dtype=jnp.int32)
    slot_of = jnp.sum(jnp.where(slot_channel[:, None] == slot_ids[None, :], slot_ids[:, None], 0), axis=0)
    vmem = pl.BlockSpec(memory_space=pltpu.VMEM)
    smem = pl.BlockSpec(memory_space=pltpu.SMEM)
    anywhere = pl.BlockSpec(memory_space=pl.ANY)
    dma = pltpu.SemaphoreType.DMA
    return pl.pallas_call(
        kernel,
        name="step",
        out_shape=jax.ShapeDtypeStruct(vectors.shape, F32),
        in_specs=[pl.BlockSpec(memory_space=pl.ANY), vmem, vmem, vmem] + [smem] * 4 + [anywhere, anywhere, smem, anywhere],
        out_specs=vmem,
        scratch_shapes=[
            pltpu.VMEM((2, POINTS, POINTS), F32),
            pltpu.VMEM((2, FULL, FULL), BF16),
            pltpu.VMEM((2, FULL, FULL), BF16),
            pltpu.VMEM((2, FULL, FULL), BF16),
            pltpu.VMEM((2, FULL, FULL), BF16),
            pltpu.VMEM((2, POINTS, POINTS), F32),
            pltpu.VMEM((FULL, POINTS), BF16),
            pltpu.VMEM((FULL, POINTS), BF16),
            pltpu.VMEM((FULL, POINTS), BF16),
            pltpu.VMEM((FULL, POINTS), BF16),
            pltpu.VMEM((2, POINTS, POINTS), F32),
            pltpu.VMEM((DEVICES, 2, 16, 128), BF16),
            pltpu.VMEM((CHANNELS, 2, 16, 128), BF16),
            pltpu.VMEM((CHANNELS, 2, 16, 128), BF16),
            pltpu.VMEM((DEVICES, 2, 16, 128), BF16),
            pltpu.VMEM((NRAD, 2, ROWS, POINTS), BF16),
            pltpu.VMEM((GROUP, 2, ROWS, POINTS), BF16),
            pltpu.VMEM((ORDERS, 2, 16, 128), F32),
            dma,
            dma((NRAD,)),
            dma,
            dma,
            dma,
            dma((4,)),
            dma,
            dma,
            pltpu.SemaphoreType.REGULAR,
            pltpu.SMEM((CHANNELS, LINKS), jnp.int32),
            pltpu.SMEM((CHANNELS, LINKS), jnp.int32),
            pltpu.SMEM((CHANNELS, LINKS), F32),
            dma((3,)),
        ],
        compiler_params=pltpu.CompilerParams(
            collective_id=0, has_side_effects=True, vmem_limit_bytes=62 * 1024 * 1024
        ),
    )(
        vectors,
        eigenvectors,
        energies.reshape(1, POINTS),
        widths.reshape(1, POINTS),
        shift_energy,
        shift_width,
        slot_channel,
        slot_of.reshape(1, CHANNELS),
        partners,
        multipole,
        counts,
        angular,
    )


def solution(mesh):
    spread = P(None, None, "chan", "rad", None)
    return jax.shard_map(
        local,
        mesh=mesh,
        in_specs=(spread,) + (P(),) * 10,
        out_specs=spread,
        check_vma=False,
    )
```

```python
import math

import jax
import jax.numpy as jnp
from jax import lax
from jax.experimental import pallas as pl
from jax.experimental.pallas import tpu as pltpu
from jax.sharding import PartitionSpec as P

F32 = jnp.float32
BF16 = jnp.bfloat16
MESH = pl.DeviceIdType.MESH
POINTS = 512
CHANNELS = 104
GROUP = 13
ORDERS = 4
LINKS = 12
NCHAN = 8
NRAD = 16
DEVICES = NCHAN * NRAD
ROWS = POINTS // NRAD
HALF = POINTS
FULL = 2 * POINTS

spacing = 0.01
first_point = 8.0
angle_ecs = 0.3


def dot(a, b):
    return jnp.dot(a, b, preferred_element_type=F32)


def split(x):
    hi = x.astype(BF16)
    return hi, (x - hi.astype(F32)).astype(BF16)


def complex_product(a, b):
    return (a[0] * b[0] - a[1] * b[1], a[0] * b[1] + a[1] * b[0])


def kernel(
    vec,
    eig,
    energies,
    widths,
    shift_energy,
    shift_width,
    slot_channel,
    slot_of,
    partners_in,
    multipole_in,
    counts,
    angular_in,
    out,
    xin,
    wr,
    wrt,
    wl,
    wlt,
    fac,
    yh,
    yl,
    zh,
    zl,
    a1,
    fb,
    got,
    csend,
    crecv,
    dsend,
    drecv,
    table,
    t1s,
    t1r,
    t2s,
    t2r,
    t3s,
    t3r,
    t4s,
    t4r,
    ready,
    partners,
    multipole,
    angular,
    tab,
):
    chan = lax.axis_index("chan")
    rad = lax.axis_index("rad")
    seat = (rad + 5 * (chan % 2)) % NRAD
    has_slot = jnp.logical_or(seat % 5 != 0, seat == 0)
    my_place = seat - seat // 5
    my_slot = chan * GROUP + my_place

    def place_of(to_chan, to_rad):
        to_seat = (to_rad + 5 * (to_chan % 2)) % NRAD
        return jnp.logical_or(to_seat % 5 != 0, to_seat == 0), to_seat - to_seat // 5

    def rad_of(to_chan, place):
        to_seat = place + jnp.where(place >= 5, 1, 0) + jnp.where(place >= 9, 1, 0)
        return (to_seat + 11 * (to_chan % 2)) % NRAD

    my_block = 32 * ((rad // 4 + rad % 4) % 4) + NCHAN * (rad % 4) + chan
    plane = rad // 4

    my_rows = pl.ds(pl.multiple_of(rad * ROWS, ROWS), ROWS)

    def left_pair(weights, right_h, right_l, m, size):
        rows = pl.ds(pl.multiple_of(m * size, size), size)
        low = pl.ds(pl.multiple_of(HALF + m * size, size), size)
        result = []
        for r in (rows, low):
            h = weights[0, r, :]
            lo = weights[1, r, :]
            result.append(dot(h, right_h[...]) + dot(h, right_l[...]) + dot(lo, right_h[...]))
        return result

    def scaled_left(m):
        size = 256
        rows = pl.ds(pl.multiple_of(m * size, size), size)
        low = pl.ds(pl.multiple_of(HALF + m * size, size), size)
        re, im = left_pair(wlt, yh, yl, m, size)
        z = complex_product((re, im), (fac[0, rows, :], fac[1, rows, :]))
        for r, v in zip((rows, low), z):
            h, lo = split(v)
            zh[r, :] = h
            zl[r, :] = lo

    def store_y(g, y):
        rows = pl.ds(pl.multiple_of(g * 128, 128), 128)
        low = pl.ds(pl.multiple_of(HALF + g * 128, 128), 128)
        h, lo = split(y)
        yh[rows, :] = h[:, 0:HALF]
        yh[low, :] = h[:, HALF:FULL]
        yl[rows, :] = lo[:, 0:HALF]
        yl[low, :] = lo[:, HALF:FULL]

    barrier = pltpu.get_barrier_semaphore()

    def greet():
        @pl.loop(1, NRAD)
        def _(k):
            to_rad = (rad + k) % NRAD
            pl.semaphore_signal(barrier, inc=1, device_id=(chan, to_rad), device_id_type=MESH)

        @pl.loop(1, NCHAN)
        def _(k):
            to_chan = (chan + k) % NCHAN
            pl.semaphore_signal(barrier, inc=1, device_id=(to_chan, rad), device_id_type=MESH)

        pl.semaphore_wait(barrier, NRAD + NCHAN - 2)

        @pl.loop(1, NCHAN)
        def _(k):
            to_chan = (chan + k) % NCHAN
            pl.semaphore_signal(ready, inc=1, device_id=(to_chan, rad), device_id_type=MESH)

    def send_rows():
        @pl.loop(0, NRAD)
        def _(k):
            s = (rad + 1 + k) % NRAD
            taken, place = place_of(chan, s)

            @pl.when(jnp.logical_and(taken, s != rad))
            def _():
                pltpu.make_async_remote_copy(
                    src_ref=vec.at[0, :, place],
                    dst_ref=xin.at[:, my_rows],
                    send_sem=t1s,
                    recv_sem=t1r.at[rad],
                    device_id=(chan, s),
                    device_id_type=MESH,
                ).start()

        @pl.when(has_slot)
        def _():
            pltpu.make_async_copy(vec.at[0, :, my_place], xin.at[:, my_rows], t1r.at[rad]).start()

    def all_ready():
        pl.semaphore_wait(ready, NCHAN - 1)

    def tables():
        return [
            pltpu.make_async_copy(partners_in, partners, tab.at[0]),
            pltpu.make_async_copy(multipole_in, multipole, tab.at[1]),
            pltpu.make_async_copy(angular_in, angular, tab.at[2]),
        ]

    def prepare():
        for copy in tables():
            copy.start()

        @pl.loop(0, 4)
        def _(g):
            rows = pl.ds(pl.multiple_of(g * 128, 128), 128)
            low = pl.ds(pl.multiple_of(HALF + g * 128, 128), 128)
            ur = eig[0, rows, :]
            ui = eig[1, rows, :]
            for part, (r, i) in enumerate(zip(split(ur), split(ui))):
                wr[part, rows, 0:HALF] = r
                wr[part, rows, HALF:FULL] = i
                wr[part, low, 0:HALF] = -i
                wr[part, low, HALF:FULL] = r
                wl[part, rows, 0:HALF] = r
                wl[part, rows, HALF:FULL] = -i
                wl[part, low, 0:HALF] = i
                wl[part, low, HALF:FULL] = r
            tr = eig[0, :, rows].T
            ti = eig[1, :, rows].T
            for part, (r, i) in enumerate(zip(split(tr), split(ti))):
                wrt[part, rows, 0:HALF] = r
                wrt[part, rows, HALF:FULL] = i
                wrt[part, low, 0:HALF] = -i
                wrt[part, low, HALF:FULL] = r
                wlt[part, rows, 0:HALF] = r
                wlt[part, rows, HALF:FULL] = -i
                wlt[part, low, 0:HALF] = i
                wlt[part, low, HALF:FULL] = r
            e_row = jnp.broadcast_to(energies[0:1, :], (128, POINTS))
            w_row = jnp.broadcast_to(widths[0:1, :], (128, POINTS))
            e_col = jnp.broadcast_to(energies[0:1, rows], (POINTS, 128)).T
            w_col = jnp.broadcast_to(widths[0:1, rows], (POINTS, 128)).T
            den_real = e_col + e_row - shift_energy[0]
            den_imag = -(w_col + w_row) - shift_width[0]
            modulus = den_real * den_real + den_imag * den_imag
            fac[0, rows, :] = den_real / modulus
            fac[1, rows, :] = -den_imag / modulus

        row = my_block // 4 * 16 + lax.broadcasted_iota(jnp.int32, (16, 128), 0)
        col = my_block % 4 * 128 + lax.broadcasted_iota(jnp.int32, (16, 128), 1)

        def bent(index):
            start = 3 * POINTS // 4
            position = spacing * (index.astype(F32) + first_point)
            edge = spacing * (start + first_point)
            beyond = jnp.maximum(position - edge, 0.0)
            return (jnp.minimum(position, edge) + beyond * math.cos(angle_ecs), beyond * math.sin(angle_ecs))

        upper = bent(jnp.maximum(row, col))
        lower = bent(jnp.minimum(row, col))
        modulus = upper[0] * upper[0] + upper[1] * upper[1]
        inverse = (upper[0] / modulus, -upper[1] / modulus)
        ratio = complex_product(lower, inverse)
        now = inverse
        for order in range(ORDERS):
            table[order, 0] = now[0]
            table[order, 1] = now[1]
            now = complex_product(now, ratio)

    def first_pass():
        @pl.when(has_slot)
        def _():
            @pl.loop(0, 4)
            def _(k):
                g = (plane + k) % 4

                @pl.loop(0, 4)
                def _(q):
                    src = 4 * g + q
                    part = xin.at[:, pl.ds(pl.multiple_of(src * ROWS, ROWS), ROWS)]
                    pltpu.make_async_copy(part, part, t1r.at[src]).wait()

                rows = pl.ds(pl.multiple_of(g * 128, 128), 128)
                x = jnp.concatenate([xin[0, rows, :], xin[1, rows, :]], axis=1)
                h, lo = split(x)
                store_y(g, dot(h, wr[0]) + dot(h, wr[1]) + dot(lo, wr[0]))

            @pl.loop(0, 2)
            def _(m):
                scaled_left(m)

            @pl.loop(0, 4)
            def _(k):
                m = (plane + 1 + k) % 4
                rows = pl.ds(pl.multiple_of(m * 128, 128), 128)
                re, im = left_pair(wl, zh, zl, m, 128)
                a1[0, rows, :] = re
                a1[1, rows, :] = im
                h, lo = split(jnp.concatenate([re, im], axis=1))
                f = (dot(h, wrt[0]) + dot(h, wrt[1]) + dot(lo, wrt[0])).astype(BF16)
                for ii in range(8):
                    for j in range(4):
                        for ri in range(2):
                            at = HALF * ri + 128 * j
                            fb[32 * m + 4 * ii + j, ri] = f[16 * ii : 16 * ii + 16, at : at + 128]

                @pl.loop(0, 32)
                def _(q):
                    d = 32 * m + q

                    @pl.when(d == my_block)
                    def _():
                        pltpu.make_async_copy(fb.at[d], got.at[my_slot], t2r).start()

                    @pl.when(d != my_block)
                    def _():
                        pltpu.make_async_remote_copy(
                            src_ref=fb.at[d],
                            dst_ref=got.at[my_slot],
                            send_sem=t2s,
                            recv_sem=t2r,
                            device_id=(q % NCHAN, 4 * ((m + 4 - q // NCHAN) % 4) + q // NCHAN),
                            device_id_type=MESH,
                        ).start()

    def couple():
        pltpu.make_async_copy(got, got, t2r).wait()

        def mixed(s):
            c = slot_channel[s]
            live = counts[c]
            re = jnp.zeros((16, 128), F32)
            im = jnp.zeros((16, 128), F32)
            for p in range(LINKS):
                w = jnp.where(p < live, angular[c, p], 0.0)
                order = multipole[c, p]
                t = slot_of[0, partners[c, p]]
                gr = w * table[order, 0]
                gi = w * table[order, 1]
                vr = got[t, 0].astype(F32)
                vi = got[t, 1].astype(F32)
                re = re + (gr * vr - gi * vi)
                im = im + (gr * vi + gi * vr)
            return re.astype(BF16), im.astype(BF16)

        @pl.loop(0, CHANNELS // 4)
        def _(k):
            slots = [(my_slot + 1 + k + CHANNELS // 4 * u) % CHANNELS for u in range(4)]
            fields = [mixed(s) for s in slots]
            for s, (re, im) in zip(slots, fields):
                csend[s, 0] = re
                csend[s, 1] = im

            @pl.loop(0, 4)
            def _(u):
                s = (my_slot + 1 + k + CHANNELS // 4 * u) % CHANNELS
                to_chan = s // GROUP
                to_rad = rad_of(to_chan, s % GROUP)
                same = jnp.logical_and(to_rad == rad, to_chan == chan)

                @pl.when(same)
                def _():
                    pltpu.make_async_copy(csend.at[s], crecv.at[my_block], t3r.at[my_block // 32]).start()

                @pl.when(jnp.logical_not(same))
                def _():
                    pltpu.make_async_remote_copy(
                        src_ref=csend.at[s],
                        dst_ref=crecv.at[my_block],
                        send_sem=t3s,
                        recv_sem=t3r.at[my_block // 32],
                        device_id=(to_chan, to_rad),
                        device_id_type=MESH,
                    ).start()

    def second_pass():
        @pl.when(has_slot)
        def _():
            @pl.loop(0, 4)
            def _(k):
                m = (plane + k) % 4
                part = crecv.at[pl.ds(pl.multiple_of(32 * m, 32), 32)]
                pltpu.make_async_copy(part, part, t3r.at[m]).wait()
                cols = []
                for ri in range(2):
                    for j in range(4):
                        cols.append(jnp.concatenate([crecv[32 * m + 4 * ii + j, ri] for ii in range(8)], axis=0))
                x = jnp.concatenate(cols, axis=1)
                store_y(m, dot(x, wr[0]) + dot(x, wr[1]))

            @pl.loop(0, 2)
            def _(m):
                scaled_left(m)

            @pl.loop(0, 4)
            def _(k):
                m = (plane + jnp.where(k == 1, 3, jnp.where(k == 2, 2, jnp.where(k == 3, 4, 1)))) % 4
                rows = pl.ds(pl.multiple_of(m * 128, 128), 128)
                re, im = left_pair(wl, zh, zl, m, 128)
                for ri, v in enumerate((re, im)):
                    diff = (a1[ri, rows, :] - v).astype(BF16)
                    for q in range(4):
                        dsend[4 * m + q, ri] = diff[ROWS * q : ROWS * q + ROWS, :]

                @pl.loop(0, 4)
                def _(q):
                    r = 4 * m + q

                    @pl.when(r == rad)
                    def _():
                        pltpu.make_async_copy(dsend.at[r], drecv.at[my_place], t4r).start()

                    @pl.when(r != rad)
                    def _():
                        pltpu.make_async_remote_copy(
                            src_ref=dsend.at[r],
                            dst_ref=drecv.at[my_place],
                            send_sem=t4s,
                            recv_sem=t4r,
                            device_id=(chan, r),
                            device_id_type=MESH,
                        ).start()

    def finish():
        pltpu.make_async_copy(drecv, drecv, t4r).wait()

        x = jnp.concatenate(
            [drecv[:, 0].reshape(GROUP * ROWS, POINTS), drecv[:, 1].reshape(GROUP * ROWS, POINTS)], axis=1
        )

        @pl.loop(0, 2)
        def _(ri):
            cols = pl.ds(pl.multiple_of(HALF * ri, HALF), HALF)
            u = dot(x, wrt[0, :, cols]) + dot(x, wrt[1, :, cols])
            out[0, ri] = u.reshape(GROUP, ROWS, POINTS)

    def drain():
        @pl.when(has_slot)
        def _():
            a = xin.at[:, pl.ds(0, (GROUP - 1) * ROWS)]
            pltpu.make_async_copy(a, a, t1s).wait()
            b = fb.at[pl.ds(0, DEVICES - 1)]
            pltpu.make_async_copy(b, b, t2s).wait()
            c = csend.at[pl.ds(0, CHANNELS - 1)]
            pltpu.make_async_copy(c, c, t3s).wait()
            d = dsend.at[pl.ds(0, NRAD - 1)]
            pltpu.make_async_copy(d, d, t4s).wait()

        @pl.when(jnp.logical_not(has_slot))
        def _():
            a = xin.at[:, pl.ds(0, GROUP * ROWS)]
            pltpu.make_async_copy(a, a, t1s).wait()
            pltpu.make_async_copy(csend, csend, t3s).wait()

    greet()
    send_rows()
    prepare()
    all_ready()
    for copy in tables():
        copy.wait()
    first_pass()
    couple()
    second_pass()
    finish()
    drain()


def local(
    vectors,
    eigenvectors,
    energies,
    widths,
    shift_energy,
    shift_width,
    slot_channel,
    partners,
    multipole,
    counts,
    angular,
):
    slot_ids = jnp.arange(CHANNELS, dtype=jnp.int32)
    slot_of = jnp.sum(jnp.where(slot_channel[:, None] == slot_ids[None, :], slot_ids[:, None], 0), axis=0)
    vmem = pl.BlockSpec(memory_space=pltpu.VMEM)
    smem = pl.BlockSpec(memory_space=pltpu.SMEM)
    anywhere = pl.BlockSpec(memory_space=pl.ANY)
    dma = pltpu.SemaphoreType.DMA
    return pl.pallas_call(
        kernel,
        name="step",
        out_shape=jax.ShapeDtypeStruct(vectors.shape, F32),
        in_specs=[pl.BlockSpec(memory_space=pl.ANY), vmem, vmem, vmem] + [smem] * 4 + [anywhere, anywhere, smem, anywhere],
        out_specs=vmem,
        scratch_shapes=[
            pltpu.VMEM((2, POINTS, POINTS), F32),
            pltpu.VMEM((2, FULL, FULL), BF16),
            pltpu.VMEM((2, FULL, FULL), BF16),
            pltpu.VMEM((2, FULL, FULL), BF16),
            pltpu.VMEM((2, FULL, FULL), BF16),
            pltpu.VMEM((2, POINTS, POINTS), F32),
            pltpu.VMEM((FULL, POINTS), BF16),
            pltpu.VMEM((FULL, POINTS), BF16),
            pltpu.VMEM((FULL, POINTS), BF16),
            pltpu.VMEM((FULL, POINTS), BF16),
            pltpu.VMEM((2, POINTS, POINTS), F32),
            pltpu.VMEM((DEVICES, 2, 16, 128), BF16),
            pltpu.VMEM((CHANNELS, 2, 16, 128), BF16),
            pltpu.VMEM((CHANNELS, 2, 16, 128), BF16),
            pltpu.VMEM((DEVICES, 2, 16, 128), BF16),
            pltpu.VMEM((NRAD, 2, ROWS, POINTS), BF16),
            pltpu.VMEM((GROUP, 2, ROWS, POINTS), BF16),
            pltpu.VMEM((ORDERS, 2, 16, 128), F32),
            dma,
            dma((NRAD,)),
            dma,
            dma,
            dma,
            dma((4,)),
            dma,
            dma,
            pltpu.SemaphoreType.REGULAR,
            pltpu.SMEM((CHANNELS, LINKS), jnp.int32),
            pltpu.SMEM((CHANNELS, LINKS), jnp.int32),
            pltpu.SMEM((CHANNELS, LINKS), F32),
            dma((3,)),
        ],
        compiler_params=pltpu.CompilerParams(
            collective_id=0, has_side_effects=True, vmem_limit_bytes=62 * 1024 * 1024
        ),
    )(
        vectors,
        eigenvectors,
        energies.reshape(1, POINTS),
        widths.reshape(1, POINTS),
        shift_energy,
        shift_width,
        slot_channel,
        slot_of.reshape(1, CHANNELS),
        partners,
        multipole,
        counts,
        angular,
    )


def solution(mesh):
    spread = P(None, None, "chan", "rad", None)
    return jax.shard_map(
        local,
        mesh=mesh,
        in_specs=(spread,) + (P(),) * 10,
        out_specs=spread,
        check_vma=False,
    )
```

```python
import math

import jax
import jax.numpy as jnp
from jax import lax
from jax.experimental import pallas as pl
from jax.experimental.pallas import tpu as pltpu
from jax.sharding import PartitionSpec as P

F32 = jnp.float32
BF16 = jnp.bfloat16
MESH = pl.DeviceIdType.MESH
POINTS = 512
CHANNELS = 104
GROUP = 13
ORDERS = 4
LINKS = 12
NCHAN = 8
NRAD = 16
DEVICES = NCHAN * NRAD
ROWS = POINTS // NRAD
HALF = POINTS
FULL = 2 * POINTS

spacing = 0.01
first_point = 8.0
angle_ecs = 0.3


def dot(a, b):
    return jnp.dot(a, b, preferred_element_type=F32)


def split(x):
    hi = x.astype(BF16)
    return hi, (x - hi.astype(F32)).astype(BF16)


def complex_product(a, b):
    return (a[0] * b[0] - a[1] * b[1], a[0] * b[1] + a[1] * b[0])


def kernel(
    vec,
    eig,
    energies,
    widths,
    shift_energy,
    shift_width,
    slot_channel,
    slot_of,
    partners_in,
    multipole_in,
    counts,
    angular_in,
    out,
    xin,
    wr,
    wrt,
    wl,
    wlt,
    fac,
    yh,
    yl,
    zh,
    zl,
    a1,
    fb,
    got,
    csend,
    crecv,
    dsend,
    drecv,
    table,
    t1s,
    t1r,
    t2s,
    t2r,
    t3s,
    t3r,
    t4s,
    t4r,
    ready,
    partners,
    multipole,
    angular,
    tab,
):
    chan = lax.axis_index("chan")
    rad = lax.axis_index("rad")
    seat = (rad + 5 * (chan % 2)) % NRAD
    has_slot = jnp.logical_or(seat % 5 != 0, seat == 0)
    my_place = seat - seat // 5
    my_slot = chan * GROUP + my_place

    def place_of(to_chan, to_rad):
        to_seat = (to_rad + 5 * (to_chan % 2)) % NRAD
        return jnp.logical_or(to_seat % 5 != 0, to_seat == 0), to_seat - to_seat // 5

    def rad_of(to_chan, place):
        to_seat = place + jnp.where(place >= 5, 1, 0) + jnp.where(place >= 9, 1, 0)
        return (to_seat + 11 * (to_chan % 2)) % NRAD

    my_block = 32 * ((rad // 4 + rad % 4) % 4) + NCHAN * (rad % 4) + chan
    plane = rad // 4

    my_rows = pl.ds(pl.multiple_of(rad * ROWS, ROWS), ROWS)

    def left_pair(weights, right_h, right_l, m, size):
        rows = pl.ds(pl.multiple_of(m * size, size), size)
        low = pl.ds(pl.multiple_of(HALF + m * size, size), size)
        result = []
        for r in (rows, low):
            h = weights[0, r, :]
            lo = weights[1, r, :]
            result.append(dot(h, right_h[...]) + dot(h, right_l[...]) + dot(lo, right_h[...]))
        return result

    def scaled_left(m):
        size = 256
        rows = pl.ds(pl.multiple_of(m * size, size), size)
        low = pl.ds(pl.multiple_of(HALF + m * size, size), size)
        re, im = left_pair(wlt, yh, yl, m, size)
        z = complex_product((re, im), (fac[0, rows, :], fac[1, rows, :]))
        for r, v in zip((rows, low), z):
            h, lo = split(v)
            zh[r, :] = h
            zl[r, :] = lo

    def store_y(g, y):
        rows = pl.ds(pl.multiple_of(g * 128, 128), 128)
        low = pl.ds(pl.multiple_of(HALF + g * 128, 128), 128)
        h, lo = split(y)
        yh[rows, :] = h[:, 0:HALF]
        yh[low, :] = h[:, HALF:FULL]
        yl[rows, :] = lo[:, 0:HALF]
        yl[low, :] = lo[:, HALF:FULL]

    barrier = pltpu.get_barrier_semaphore()

    def greet():
        @pl.loop(1, NRAD)
        def _(k):
            to_rad = (rad + k) % NRAD
            pl.semaphore_signal(barrier, inc=1, device_id=(chan, to_rad), device_id_type=MESH)

        @pl.loop(1, NCHAN)
        def _(k):
            to_chan = (chan + k) % NCHAN
            pl.semaphore_signal(barrier, inc=1, device_id=(to_chan, rad), device_id_type=MESH)

        pl.semaphore_wait(barrier, NRAD + NCHAN - 2)

        @pl.loop(1, NCHAN)
        def _(k):
            to_chan = (chan + k) % NCHAN
            pl.semaphore_signal(ready, inc=1, device_id=(to_chan, rad), device_id_type=MESH)

    def send_rows():
        @pl.loop(0, NRAD)
        def _(k):
            s = (rad + 1 + k) % NRAD
            taken, place = place_of(chan, s)

            @pl.when(jnp.logical_and(taken, s != rad))
            def _():
                pltpu.make_async_remote_copy(
                    src_ref=vec.at[0, :, place],
                    dst_ref=xin.at[:, my_rows],
                    send_sem=t1s,
                    recv_sem=t1r.at[rad],
                    device_id=(chan, s),
                    device_id_type=MESH,
                ).start()

        @pl.when(has_slot)
        def _():
            pltpu.make_async_copy(vec.at[0, :, my_place], xin.at[:, my_rows], t1r.at[rad]).start()

    def all_ready():
        pl.semaphore_wait(ready, NCHAN - 1)

    def tables():
        return [
            pltpu.make_async_copy(partners_in, partners, tab.at[0]),
            pltpu.make_async_copy(multipole_in, multipole, tab.at[1]),
            pltpu.make_async_copy(angular_in, angular, tab.at[2]),
        ]

    def prepare():
        for copy in tables():
            copy.start()

        @pl.loop(0, 4)
        def _(g):
            rows = pl.ds(pl.multiple_of(g * 128, 128), 128)
            low = pl.ds(pl.multiple_of(HALF + g * 128, 128), 128)
            ur = eig[0, rows, :]
            ui = eig[1, rows, :]
            for part, (r, i) in enumerate(zip(split(ur), split(ui))):
                wr[part, rows, 0:HALF] = r
                wr[part, rows, HALF:FULL] = i
                wr[part, low, 0:HALF] = -i
                wr[part, low, HALF:FULL] = r
                wl[part, rows, 0:HALF] = r
                wl[part, rows, HALF:FULL] = -i
                wl[part, low, 0:HALF] = i
                wl[part, low, HALF:FULL] = r
            tr = eig[0, :, rows].T
            ti = eig[1, :, rows].T
            for part, (r, i) in enumerate(zip(split(tr), split(ti))):
                wrt[part, rows, 0:HALF] = r
                wrt[part, rows, HALF:FULL] = i
                wrt[part, low, 0:HALF] = -i
                wrt[part, low, HALF:FULL] = r
                wlt[part, rows, 0:HALF] = r
                wlt[part, rows, HALF:FULL] = -i
                wlt[part, low, 0:HALF] = i
                wlt[part, low, HALF:FULL] = r
            e_row = jnp.broadcast_to(energies[0:1, :], (128, POINTS))
            w_row = jnp.broadcast_to(widths[0:1, :], (128, POINTS))
            e_col = jnp.broadcast_to(energies[0:1, rows], (POINTS, 128)).T
            w_col = jnp.broadcast_to(widths[0:1, rows], (POINTS, 128)).T
            den_real = e_col + e_row - shift_energy[0]
            den_imag = -(w_col + w_row) - shift_width[0]
            modulus = den_real * den_real + den_imag * den_imag
            fac[0, rows, :] = den_real / modulus
            fac[1, rows, :] = -den_imag / modulus

        row = my_block // 4 * 16 + lax.broadcasted_iota(jnp.int32, (16, 128), 0)
        col = my_block % 4 * 128 + lax.broadcasted_iota(jnp.int32, (16, 128), 1)

        def bent(index):
            start = 3 * POINTS // 4
            position = spacing * (index.astype(F32) + first_point)
            edge = spacing * (start + first_point)
            beyond = jnp.maximum(position - edge, 0.0)
            return (jnp.minimum(position, edge) + beyond * math.cos(angle_ecs), beyond * math.sin(angle_ecs))

        upper = bent(jnp.maximum(row, col))
        lower = bent(jnp.minimum(row, col))
        modulus = upper[0] * upper[0] + upper[1] * upper[1]
        inverse = (upper[0] / modulus, -upper[1] / modulus)
        ratio = complex_product(lower, inverse)
        now = inverse
        for order in range(ORDERS):
            table[order, 0] = now[0]
            table[order, 1] = now[1]
            now = complex_product(now, ratio)

    def first_pass():
        @pl.when(has_slot)
        def _():
            @pl.loop(0, 4)
            def _(k):
                g = (plane + k) % 4

                @pl.loop(0, 4)
                def _(q):
                    src = 4 * g + q
                    part = xin.at[:, pl.ds(pl.multiple_of(src * ROWS, ROWS), ROWS)]
                    pltpu.make_async_copy(part, part, t1r.at[src]).wait()

                rows = pl.ds(pl.multiple_of(g * 128, 128), 128)
                x = jnp.concatenate([xin[0, rows, :], xin[1, rows, :]], axis=1)
                h, lo = split(x)
                store_y(g, dot(h, wr[0]) + dot(h, wr[1]) + dot(lo, wr[0]))

            @pl.loop(0, 2)
            def _(m):
                scaled_left(m)

            @pl.loop(0, 4)
            def _(k):
                m = (plane + 1 + k) % 4
                rows = pl.ds(pl.multiple_of(m * 128, 128), 128)
                re, im = left_pair(wl, zh, zl, m, 128)
                a1[0, rows, :] = re
                a1[1, rows, :] = im
                h, lo = split(jnp.concatenate([re, im], axis=1))
                f = (dot(h, wrt[0]) + dot(h, wrt[1]) + dot(lo, wrt[0])).astype(BF16)
                for ii in range(8):
                    for j in range(4):
                        for ri in range(2):
                            at = HALF * ri + 128 * j
                            fb[32 * m + 4 * ii + j, ri] = f[16 * ii : 16 * ii + 16, at : at + 128]

                @pl.loop(0, 32)
                def _(turn):
                    q = (turn + my_slot) % 32
                    d = 32 * m + q

                    @pl.when(d == my_block)
                    def _():
                        pltpu.make_async_copy(fb.at[d], got.at[my_slot], t2r).start()

                    @pl.when(d != my_block)
                    def _():
                        pltpu.make_async_remote_copy(
                            src_ref=fb.at[d],
                            dst_ref=got.at[my_slot],
                            send_sem=t2s,
                            recv_sem=t2r,
                            device_id=(q % NCHAN, 4 * ((m + 4 - q // NCHAN) % 4) + q // NCHAN),
                            device_id_type=MESH,
                        ).start()

    def couple():
        pltpu.make_async_copy(got, got, t2r).wait()

        def mixed(s):
            c = slot_channel[s]
            live = counts[c]
            re = jnp.zeros((16, 128), F32)
            im = jnp.zeros((16, 128), F32)
            for p in range(LINKS):
                w = jnp.where(p < live, angular[c, p], 0.0)
                order = multipole[c, p]
                t = slot_of[0, partners[c, p]]
                gr = w * table[order, 0]
                gi = w * table[order, 1]
                vr = got[t, 0].astype(F32)
                vi = got[t, 1].astype(F32)
                re = re + (gr * vr - gi * vi)
                im = im + (gr * vi + gi * vr)
            return re.astype(BF16), im.astype(BF16)

        @pl.loop(0, CHANNELS // 4)
        def _(k):
            slots = [(my_slot + 1 + k + CHANNELS // 4 * u) % CHANNELS for u in range(4)]
            fields = [mixed(s) for s in slots]
            for s, (re, im) in zip(slots, fields):
                csend[s, 0] = re
                csend[s, 1] = im

            @pl.loop(0, 4)
            def _(u):
                s = (my_slot + 1 + k + CHANNELS // 4 * u) % CHANNELS
                to_chan = s // GROUP
                to_rad = rad_of(to_chan, s % GROUP)
                same = jnp.logical_and(to_rad == rad, to_chan == chan)

                @pl.when(same)
                def _():
                    pltpu.make_async_copy(csend.at[s], crecv.at[my_block], t3r.at[my_block // 32]).start()

                @pl.when(jnp.logical_not(same))
                def _():
                    pltpu.make_async_remote_copy(
                        src_ref=csend.at[s],
                        dst_ref=crecv.at[my_block],
                        send_sem=t3s,
                        recv_sem=t3r.at[my_block // 32],
                        device_id=(to_chan, to_rad),
                        device_id_type=MESH,
                    ).start()

    def second_pass():
        @pl.when(has_slot)
        def _():
            @pl.loop(0, 4)
            def _(k):
                m = (plane + k) % 4
                part = crecv.at[pl.ds(pl.multiple_of(32 * m, 32), 32)]
                pltpu.make_async_copy(part, part, t3r.at[m]).wait()
                cols = []
                for ri in range(2):
                    for j in range(4):
                        cols.append(jnp.concatenate([crecv[32 * m + 4 * ii + j, ri] for ii in range(8)], axis=0))
                x = jnp.concatenate(cols, axis=1)
                store_y(m, dot(x, wr[0]) + dot(x, wr[1]))

            @pl.loop(0, 2)
            def _(m):
                scaled_left(m)

            @pl.loop(0, 4)
            def _(k):
                m = (plane + jnp.where(k == 1, 3, jnp.where(k == 2, 2, jnp.where(k == 3, 4, 1)))) % 4
                rows = pl.ds(pl.multiple_of(m * 128, 128), 128)
                re, im = left_pair(wl, zh, zl, m, 128)
                for ri, v in enumerate((re, im)):
                    diff = (a1[ri, rows, :] - v).astype(BF16)
                    for q in range(4):
                        dsend[4 * m + q, ri] = diff[ROWS * q : ROWS * q + ROWS, :]

                @pl.loop(0, 4)
                def _(turn):
                    r = 4 * m + (turn + rad + 1) % 4

                    @pl.when(r == rad)
                    def _():
                        pltpu.make_async_copy(dsend.at[r], drecv.at[my_place], t4r).start()

                    @pl.when(r != rad)
                    def _():
                        pltpu.make_async_remote_copy(
                            src_ref=dsend.at[r],
                            dst_ref=drecv.at[my_place],
                            send_sem=t4s,
                            recv_sem=t4r,
                            device_id=(chan, r),
                            device_id_type=MESH,
                        ).start()

    def finish():
        pltpu.make_async_copy(drecv, drecv, t4r).wait()

        x = jnp.concatenate(
            [drecv[:, 0].reshape(GROUP * ROWS, POINTS), drecv[:, 1].reshape(GROUP * ROWS, POINTS)], axis=1
        )

        @pl.loop(0, 2)
        def _(ri):
            cols = pl.ds(pl.multiple_of(HALF * ri, HALF), HALF)
            u = dot(x, wrt[0, :, cols]) + dot(x, wrt[1, :, cols])
            out[0, ri] = u.reshape(GROUP, ROWS, POINTS)

    def drain():
        @pl.when(has_slot)
        def _():
            a = xin.at[:, pl.ds(0, (GROUP - 1) * ROWS)]
            pltpu.make_async_copy(a, a, t1s).wait()
            b = fb.at[pl.ds(0, DEVICES - 1)]
            pltpu.make_async_copy(b, b, t2s).wait()
            c = csend.at[pl.ds(0, CHANNELS - 1)]
            pltpu.make_async_copy(c, c, t3s).wait()
            d = dsend.at[pl.ds(0, NRAD - 1)]
            pltpu.make_async_copy(d, d, t4s).wait()

        @pl.when(jnp.logical_not(has_slot))
        def _():
            a = xin.at[:, pl.ds(0, GROUP * ROWS)]
            pltpu.make_async_copy(a, a, t1s).wait()
            pltpu.make_async_copy(csend, csend, t3s).wait()

    greet()
    send_rows()
    prepare()
    all_ready()
    for copy in tables():
        copy.wait()
    first_pass()
    couple()
    second_pass()
    finish()
    drain()


def local(
    vectors,
    eigenvectors,
    energies,
    widths,
    shift_energy,
    shift_width,
    slot_channel,
    partners,
    multipole,
    counts,
    angular,
):
    slot_ids = jnp.arange(CHANNELS, dtype=jnp.int32)
    slot_of = jnp.sum(jnp.where(slot_channel[:, None] == slot_ids[None, :], slot_ids[:, None], 0), axis=0)
    vmem = pl.BlockSpec(memory_space=pltpu.VMEM)
    smem = pl.BlockSpec(memory_space=pltpu.SMEM)
    anywhere = pl.BlockSpec(memory_space=pl.ANY)
    dma = pltpu.SemaphoreType.DMA
    return pl.pallas_call(
        kernel,
        name="step",
        out_shape=jax.ShapeDtypeStruct(vectors.shape, F32),
        in_specs=[pl.BlockSpec(memory_space=pl.ANY), vmem, vmem, vmem] + [smem] * 4 + [anywhere, anywhere, smem, anywhere],
        out_specs=vmem,
        scratch_shapes=[
            pltpu.VMEM((2, POINTS, POINTS), F32),
            pltpu.VMEM((2, FULL, FULL), BF16),
            pltpu.VMEM((2, FULL, FULL), BF16),
            pltpu.VMEM((2, FULL, FULL), BF16),
            pltpu.VMEM((2, FULL, FULL), BF16),
            pltpu.VMEM((2, POINTS, POINTS), F32),
            pltpu.VMEM((FULL, POINTS), BF16),
            pltpu.VMEM((FULL, POINTS), BF16),
            pltpu.VMEM((FULL, POINTS), BF16),
            pltpu.VMEM((FULL, POINTS), BF16),
            pltpu.VMEM((2, POINTS, POINTS), F32),
            pltpu.VMEM((DEVICES, 2, 16, 128), BF16),
            pltpu.VMEM((CHANNELS, 2, 16, 128), BF16),
            pltpu.VMEM((CHANNELS, 2, 16, 128), BF16),
            pltpu.VMEM((DEVICES, 2, 16, 128), BF16),
            pltpu.VMEM((NRAD, 2, ROWS, POINTS), BF16),
            pltpu.VMEM((GROUP, 2, ROWS, POINTS), BF16),
            pltpu.VMEM((ORDERS, 2, 16, 128), F32),
            dma,
            dma((NRAD,)),
            dma,
            dma,
            dma,
            dma((4,)),
            dma,
            dma,
            pltpu.SemaphoreType.REGULAR,
            pltpu.SMEM((CHANNELS, LINKS), jnp.int32),
            pltpu.SMEM((CHANNELS, LINKS), jnp.int32),
            pltpu.SMEM((CHANNELS, LINKS), F32),
            dma((3,)),
        ],
        compiler_params=pltpu.CompilerParams(
            collective_id=0, has_side_effects=True, vmem_limit_bytes=62 * 1024 * 1024
        ),
    )(
        vectors,
        eigenvectors,
        energies.reshape(1, POINTS),
        widths.reshape(1, POINTS),
        shift_energy,
        shift_width,
        slot_channel,
        slot_of.reshape(1, CHANNELS),
        partners,
        multipole,
        counts,
        angular,
    )


def solution(mesh):
    spread = P(None, None, "chan", "rad", None)
    return jax.shard_map(
        local,
        mesh=mesh,
        in_specs=(spread,) + (P(),) * 10,
        out_specs=spread,
        check_vma=False,
    )
```
